512 devices in a mesh: blk: 32 (over z, x_hi), bfly: 16 (over y, x_lo, core).
Axes of the slice: x: 4 (x_hi: 2, x_lo: 2; x = x_hi * 2 + x_lo), y: 4, z: 16, core: 2. Of those that a mesh axis runs over, the one named last changes fastest.
Arguments:
- port_vectors: bfloat16 [32, 16, 768, 128], P('blk', 'bfly'), may hold values from -6 to 6
- column_leaf: bfloat16 [32, 16, 384, 768], P('blk', 'bfly'), may hold values from -0.21875 to 0.21875
- transfer: bfloat16 [32, 4, 16, 384, 768], P('blk', None, 'bfly'), may hold values from -0.21875 to 0.21875
- row_leaf: bfloat16 [32, 16, 768, 384], P('blk', 'bfly'), may hold values from -0.3125 to 0.3125
Outputs:
- field: bfloat16 [16, 768, 128], P('bfly', 'blk')
The draws below stay inside these ranges and needn't reach their ends.
All inputs are finite; a program needn't handle non-finite values.
Results may differ from the reference program's by a relative error of at most 0.0095.
Values may be sent and summed in bfloat16 or wider, within the bound.
No kernel may reach another device: no remote copies, remote signals or barrier semaphores. Data moves between devices by JAX's collectives and lax.ppermute only.
A program may use at most 64 MiB of HBM per device.

```python
import math
import jax
import jax.numpy as jnp
import numpy as np
from jax import lax

RANK = 384
LEAF = 768
PORTS = 128
LEVELS = 4
BLOCKS = 32
N_BLK = 32
N_BFLY = 16


def steps_of(stream_key, dims, pieces, smallest, high):
    gain = 1.0
    for axis_at, parts in pieces:
        steps = jax.random.uniform(jax.random.fold_in(jax.random.fold_in(stream_key, 6), axis_at), (parts,), jnp.float32, smallest / len(pieces), high / len(pieces))
        gain = gain * jnp.repeat(jnp.exp(steps), dims[axis_at] // parts).reshape((-1,) + (1,) * (len(dims) - 1 - axis_at))
    return gain


def bell_draw(rng, shape, scale, reach, split=(), kind=jnp.bfloat16):
    array = scale * jax.random.normal(rng, shape, jnp.float32)
    if split:
        array = array * steps_of(rng, shape, split, -0.22, 0.18)
    return jnp.clip(array, -reach, reach).astype(kind)


def setup_inputs(seed: int = 0) -> dict:
    seeds = jax.random.split(jax.random.key(seed), 5)
    return {
        "port_vectors": bell_draw(seeds[0], (BLOCKS, N_BFLY, LEAF, PORTS), 1.0, 6.0, ((0, 32), (1, 16))),
        "column_leaf": bell_draw(seeds[1], (BLOCKS, N_BFLY, RANK, LEAF), LEAF ** -0.5, 0.21875, ((0, 32), (1, 16))),
        "transfer": bell_draw(seeds[2], (BLOCKS, LEVELS, N_BFLY, RANK, 2 * RANK), (2 * RANK) ** -0.5, 0.21875, ((0, 32), (2, 16))),
        "row_leaf": bell_draw(seeds[3], (BLOCKS, N_BFLY, LEAF, RANK), RANK ** -0.5, 0.3125, ((0, 32), (1, 16))),
    }


def reference(port_vectors, column_leaf, transfer, row_leaf):
    bit_count = N_BFLY.bit_length() - 1
    positions = np.arange(N_BFLY)

    def one_block(total, items):
        ports, cleaf, trans, rleaf = items
        state = jnp.einsum('pkl,plr->pkr', cleaf.astype(jnp.float32), ports.astype(jnp.float32)).astype(jnp.bfloat16)
        for level in range(LEVELS):
            stride = 1 << level % bit_count
            lower = jnp.asarray(positions & ~stride, dtype=jnp.int32)
            upper = jnp.asarray(positions | stride, dtype=jnp.int32)
            stacked = jnp.concatenate([state[lower], state[upper]], axis=1)
            state = jnp.einsum('pkj,pjr->pkr', trans[level].astype(jnp.float32), stacked.astype(jnp.float32)).astype(jnp.bfloat16)
        partial_rows = jnp.einsum('plk,pkr->plr', rleaf.astype(jnp.float32), state.astype(jnp.float32))
        return (total + partial_rows, None)
    start = jnp.zeros((N_BFLY, LEAF, PORTS), jnp.float32)
    total, _ = lax.scan(one_block, start, (port_vectors, column_leaf, transfer, row_leaf))
    return (total * (1.0 / math.sqrt(N_BLK))).astype(jnp.bfloat16)
```

```python
import math

import jax
import jax.numpy as jnp
from jax import lax
from jax.sharding import PartitionSpec as P


def with_partner(array, axis, bit):
    pairs = [[i, i | 1 << bit] for i in range(lax.axis_size(axis)) if not i >> bit & 1]
    return lax.all_gather(array, axis, axis_index_groups=pairs, tiled=True)


def sent_and_summed(array, axis):
    count = lax.axis_size(axis)
    tiles = array.reshape(count, -1, array.shape[1])
    tiles = lax.all_to_all(tiles, axis, 0, 0, tiled=True)
    return jnp.sum(tiles.astype(jnp.float32), axis=0)


def local(port_vectors, column_leaf, transfer, row_leaf):
    bit_count = lax.axis_size("bfly").bit_length() - 1
    state = jnp.dot(
        column_leaf[0, 0], port_vectors[0, 0], preferred_element_type=jnp.float32
    ).astype(jnp.bfloat16)
    for level in range(transfer.shape[1]):
        stacked = with_partner(state, "bfly", level % bit_count)
        state = jnp.dot(
            transfer[0, level, 0], stacked, preferred_element_type=jnp.float32
        ).astype(jnp.bfloat16)
    partial_rows = jnp.dot(row_leaf[0, 0], state, preferred_element_type=jnp.float32)
    summed = sent_and_summed(partial_rows.astype(jnp.bfloat16), "blk")
    scaled = summed * (1.0 / math.sqrt(lax.axis_size("blk")))
    return scaled.astype(jnp.bfloat16)[None]


def solution(mesh):
    placed = (
        P("blk", "bfly", None, None),
        P("blk", "bfly", None, None),
        P("blk", None, "bfly", None, None),
        P("blk", "bfly", None, None),
    )
    return jax.shard_map(
        local, mesh=mesh, in_specs=placed, out_specs=P("bfly", "blk", None), check_vma=False
    )
```

```python
import functools
import math

import jax
import jax.numpy as jnp
from jax import lax
from jax.experimental import pallas as pl
from jax.experimental.pallas import tpu as pltpu
from jax.sharding import PartitionSpec as P

VMEM = pl.BlockSpec(memory_space=pltpu.VMEM)


def rows_kernel(shift, state, leaf, out):
    rows = leaf.shape[2]
    product = jnp.dot(leaf[0, 0], state[...], preferred_element_type=jnp.float32)
    product = product.astype(out.dtype)
    out[: rows - shift] = product[shift:]
    out[rows - shift :] = product[:shift]


def partial_rows(state, leaf, shift):
    return pl.pallas_call(
        functools.partial(rows_kernel, shift),
        out_shape=jax.ShapeDtypeStruct((leaf.shape[2], state.shape[1]), jnp.bfloat16),
        in_specs=[VMEM, VMEM],
        out_specs=VMEM,
        compiler_params=pltpu.CompilerParams(vmem_limit_bytes=8 << 20),
        name="partial_rows",
    )(state, leaf)


def with_partner(array, axis, bit):
    pairs = [[i, i | 1 << bit] for i in range(lax.axis_size(axis)) if not i >> bit & 1]
    return lax.all_gather(array, axis, axis_index_groups=pairs, tiled=True)


def local(port_vectors, column_leaf, transfer, row_leaf):
    bit_count = lax.axis_size("bfly").bit_length() - 1
    count = lax.axis_size("blk")
    state = jnp.dot(
        column_leaf[0, 0], port_vectors[0, 0], preferred_element_type=jnp.float32
    ).astype(jnp.bfloat16)
    for level in range(transfer.shape[1]):
        stacked = with_partner(state, "bfly", level % bit_count)
        state = jnp.dot(
            transfer[0, level, 0], stacked, preferred_element_type=jnp.float32
        ).astype(jnp.bfloat16)
    start = count // 2
    order = [(i + start) % count for i in range(count)]
    owned = row_leaf.shape[2] // count
    tiles = partial_rows(state, row_leaf, start * owned).reshape(count, owned, -1)
    tiles = lax.all_to_all(tiles, "blk", 0, 0, axis_index_groups=[order], tiled=True)
    summed = jnp.sum(tiles.astype(jnp.float32), axis=0)
    return (summed * (1.0 / math.sqrt(count))).astype(jnp.bfloat16)[None]


def solution(mesh):
    placed = (
        P("blk", "bfly", None, None),
        P("blk", "bfly", None, None),
        P("blk", None, "bfly", None, None),
        P("blk", "bfly", None, None),
    )
    return jax.shard_map(
        local, mesh=mesh, in_specs=placed, out_specs=P("bfly", "blk", None), check_vma=False
    )
```

```python
import functools
import math

import jax
import jax.numpy as jnp
from jax import lax
from jax.experimental import pallas as pl
from jax.experimental.pallas import tpu as pltpu
from jax.sharding import PartitionSpec as P

VMEM = pl.BlockSpec(memory_space=pltpu.VMEM)
HBM = pl.BlockSpec(memory_space=pltpu.HBM)


def leaf_kernel(ports, leaf, transfer, state, first, ports_v, leaf_v, sems):
    copies = [
        pltpu.make_async_copy(leaf.at[0, 0], leaf_v, sems.at[0]),
        pltpu.make_async_copy(ports.at[0, 0], ports_v, sems.at[1]),
        pltpu.make_async_copy(transfer.at[0, 0, 0], first, sems.at[2]),
    ]
    for copy in copies:
        copy.start()
    copies[0].wait()
    copies[1].wait()
    state[...] = jnp.dot(
        leaf_v[...], ports_v[...], preferred_element_type=jnp.float32
    ).astype(state.dtype)
    copies[2].wait()


def leaf_state(ports, leaf, transfer):
    rank = leaf.shape[2]
    held = [
        pltpu.with_memory_space_constraint(x, pltpu.HBM) for x in (ports, leaf, transfer)
    ]
    return pl.pallas_call(
        leaf_kernel,
        out_shape=(
            jax.ShapeDtypeStruct((rank, ports.shape[3]), jnp.bfloat16),
            jax.ShapeDtypeStruct(transfer.shape[3:], jnp.bfloat16),
        ),
        in_specs=[HBM] * 3,
        out_specs=(VMEM, VMEM),
        scratch_shapes=[
            pltpu.VMEM(ports.shape[2:], jnp.bfloat16),
            pltpu.VMEM(leaf.shape[2:], jnp.bfloat16),
            pltpu.SemaphoreType.DMA((3,)),
        ],
        compiler_params=pltpu.CompilerParams(vmem_limit_bytes=8 << 20),
        name="leaf_state",
    )(*held)


def rows_kernel(shift, state, leaf, out):
    rows = leaf.shape[2]
    product = jnp.dot(leaf[0, 0], state[...], preferred_element_type=jnp.float32)
    product = product.astype(out.dtype)
    out[: rows - shift] = product[shift:]
    out[rows - shift :] = product[:shift]


def partial_rows(state, leaf, shift):
    return pl.pallas_call(
        functools.partial(rows_kernel, shift),
        out_shape=jax.ShapeDtypeStruct((leaf.shape[2], state.shape[1]), jnp.bfloat16),
        in_specs=[VMEM, VMEM],
        out_specs=VMEM,
        compiler_params=pltpu.CompilerParams(vmem_limit_bytes=8 << 20),
        name="partial_rows",
    )(state, leaf)


def with_partner(array, axis, bit):
    pairs = [[i, i | 1 << bit] for i in range(lax.axis_size(axis)) if not i >> bit & 1]
    return lax.all_gather(array, axis, axis_index_groups=pairs, tiled=True)


def local(port_vectors, column_leaf, transfer, row_leaf):
    bit_count = lax.axis_size("bfly").bit_length() - 1
    count = lax.axis_size("blk")
    state, first = leaf_state(port_vectors, column_leaf, transfer)
    state, transfer, row_leaf = lax.optimization_barrier((state, transfer, row_leaf))
    for level in range(transfer.shape[1]):
        stacked = with_partner(state, "bfly", level % bit_count)
        matrix = transfer[0, level, 0] if level else first
        state = jnp.dot(matrix, stacked, preferred_element_type=jnp.float32)
        state = state.astype(jnp.bfloat16)
    start = count // 2
    order = [(i + start) % count for i in range(count)]
    owned = row_leaf.shape[2] // count
    tiles = partial_rows(state, row_leaf, start * owned).reshape(count, owned, -1)
    tiles = lax.all_to_all(tiles, "blk", 0, 0, axis_index_groups=[order], tiled=True)
    summed = jnp.sum(tiles.astype(jnp.float32), axis=0)
    return (summed * (1.0 / math.sqrt(count))).astype(jnp.bfloat16)[None]


def solution(mesh):
    placed = (
        P("blk", "bfly", None, None),
        P("blk", "bfly", None, None),
        P("blk", None, "bfly", None, None),
        P("blk", "bfly", None, None),
    )
    return jax.shard_map(
        local, mesh=mesh, in_specs=placed, out_specs=P("bfly", "blk", None), check_vma=False
    )
```

```python
import functools
import math

import jax
import jax.numpy as jnp
from jax import lax
from jax.experimental import pallas as pl
from jax.experimental.pallas import tpu as pltpu
from jax.sharding import PartitionSpec as P

VMEM = pl.BlockSpec(memory_space=pltpu.VMEM)
HBM = pl.BlockSpec(memory_space=pltpu.HBM)


def leaf_kernel(ports, leaf, transfer, state, first, ports_v, leaf_v, sems):
    copies = [
        pltpu.make_async_copy(leaf.at[0, 0], leaf_v, sems.at[0]),
        pltpu.make_async_copy(ports.at[0, 0], ports_v, sems.at[1]),
        pltpu.make_async_copy(transfer.at[0, 0, 0], first, sems.at[2]),
    ]
    for copy in copies:
        copy.start()
    copies[0].wait()
    copies[1].wait()
    state[...] = jnp.dot(
        leaf_v[...], ports_v[...], preferred_element_type=jnp.float32
    ).astype(state.dtype)
    copies[2].wait()


def leaf_state(ports, leaf, transfer):
    rank = leaf.shape[2]
    held = [
        pltpu.with_memory_space_constraint(x, pltpu.HBM) for x in (ports, leaf, transfer)
    ]
    return pl.pallas_call(
        leaf_kernel,
        out_shape=(
            jax.ShapeDtypeStruct((rank, ports.shape[3]), jnp.bfloat16),
            jax.ShapeDtypeStruct(transfer.shape[3:], jnp.bfloat16),
        ),
        in_specs=[HBM] * 3,
        out_specs=(VMEM, VMEM),
        scratch_shapes=[
            pltpu.VMEM(ports.shape[2:], jnp.bfloat16),
            pltpu.VMEM(leaf.shape[2:], jnp.bfloat16),
            pltpu.SemaphoreType.DMA((3,)),
        ],
        compiler_params=pltpu.CompilerParams(vmem_limit_bytes=8 << 20),
        name="leaf_state",
    )(*held)


def rows_kernel(shift, state, leaf, out):
    rows = leaf.shape[2]
    product = jnp.dot(leaf[0, 0], state[...], preferred_element_type=jnp.float32)
    product = product.astype(out.dtype)
    out[: rows - shift] = product[shift:]
    out[rows - shift :] = product[:shift]


def partial_rows(state, leaf, shift):
    return pl.pallas_call(
        functools.partial(rows_kernel, shift),
        out_shape=jax.ShapeDtypeStruct((leaf.shape[2], state.shape[1]), jnp.bfloat16),
        in_specs=[VMEM, VMEM],
        out_specs=VMEM,
        compiler_params=pltpu.CompilerParams(vmem_limit_bytes=8 << 20),
        name="partial_rows",
    )(state, leaf)


def with_partner(array, axis, bit):
    pairs = [[i, i | 1 << bit] for i in range(lax.axis_size(axis)) if not i >> bit & 1]
    return lax.all_gather(array, axis, axis_index_groups=pairs, tiled=True)


def local(port_vectors, column_leaf, transfer, row_leaf):
    bit_count = lax.axis_size("bfly").bit_length() - 1
    count = lax.axis_size("blk")
    state, first = leaf_state(port_vectors, column_leaf, transfer)
    state, transfer, row_leaf = lax.optimization_barrier((state, transfer, row_leaf))
    for level in range(transfer.shape[1]):
        stacked = with_partner(state, "bfly", level % bit_count)
        matrix = transfer[0, level, 0] if level else first
        state = jnp.dot(matrix, stacked, preferred_element_type=jnp.float32)
        state = state.astype(jnp.bfloat16)
    start = count * 5 // 8
    order = [(i + start) % count for i in range(count)]
    owned = row_leaf.shape[2] // count
    tiles = partial_rows(state, row_leaf, start * owned).reshape(count, owned, -1)
    tiles = lax.all_to_all(tiles, "blk", 0, 0, axis_index_groups=[order], tiled=True)
    summed = jnp.sum(tiles.astype(jnp.float32), axis=0)
    return (summed * (1.0 / math.sqrt(count))).astype(jnp.bfloat16)[None]


def solution(mesh):
    placed = (
        P("blk", "bfly", None, None),
        P("blk", "bfly", None, None),
        P("blk", None, "bfly", None, None),
        P("blk", "bfly", None, None),
    )
    return jax.shard_map(
        local, mesh=mesh, in_specs=placed, out_specs=P("bfly", "blk", None), check_vma=False
    )
```

```python
import functools
import math

import jax
import jax.numpy as jnp
from jax import lax
from jax.experimental import pallas as pl
from jax.experimental.pallas import tpu as pltpu
from jax.sharding import PartitionSpec as P

VMEM = pl.BlockSpec(memory_space=pltpu.VMEM)
HBM = pl.BlockSpec(memory_space=pltpu.HBM)


def leaf_kernel(ports, leaf, transfer, state, first, ports_v, leaf_v, sems):
    copies = [
        pltpu.make_async_copy(leaf.at[0, 0], leaf_v, sems.at[0]),
        pltpu.make_async_copy(ports.at[0, 0], ports_v, sems.at[1]),
        pltpu.make_async_copy(transfer.at[0, 0, 0], first, sems.at[2]),
    ]
    for copy in copies:
        copy.start()
    copies[0].wait()
    copies[1].wait()
    state[...] = jnp.dot(
        leaf_v[...], ports_v[...], preferred_element_type=jnp.float32
    ).astype(state.dtype)
    copies[2].wait()


def leaf_state(ports, leaf, transfer):
    rank = leaf.shape[2]
    held = [
        pltpu.with_memory_space_constraint(x, pltpu.HBM) for x in (ports, leaf, transfer)
    ]
    return pl.pallas_call(
        leaf_kernel,
        out_shape=(
            jax.ShapeDtypeStruct((rank, ports.shape[3]), jnp.bfloat16),
            jax.ShapeDtypeStruct(transfer.shape[3:], jnp.bfloat16),
        ),
        in_specs=[HBM] * 3,
        out_specs=(VMEM, VMEM),
        scratch_shapes=[
            pltpu.VMEM(ports.shape[2:], jnp.bfloat16),
            pltpu.VMEM(leaf.shape[2:], jnp.bfloat16),
            pltpu.SemaphoreType.DMA((3,)),
        ],
        compiler_params=pltpu.CompilerParams(vmem_limit_bytes=8 << 20),
        name="leaf_state",
    )(*held)


def rows_kernel(shift, state, leaf, out):
    rows = leaf.shape[2]
    product = jnp.dot(leaf[0, 0], state[...], preferred_element_type=jnp.float32)
    out[: rows - shift] = product[shift:].astype(out.dtype)
    out[rows - shift :] = product[:shift].astype(out.dtype)


def partial_rows(state, leaf, shift):
    return pl.pallas_call(
        functools.partial(rows_kernel, shift),
        out_shape=jax.ShapeDtypeStruct((leaf.shape[2], state.shape[1]), jnp.bfloat16),
        in_specs=[VMEM, VMEM],
        out_specs=VMEM,
        compiler_params=pltpu.CompilerParams(vmem_limit_bytes=8 << 20),
        name="partial_rows",
    )(state, leaf)


def with_partner(array, axis, bit):
    pairs = [[i, i | 1 << bit] for i in range(lax.axis_size(axis)) if not i >> bit & 1]
    return lax.all_gather(array, axis, axis_index_groups=pairs, tiled=True)


def local(port_vectors, column_leaf, transfer, row_leaf):
    bit_count = lax.axis_size("bfly").bit_length() - 1
    count = lax.axis_size("blk")
    state, first = leaf_state(port_vectors, column_leaf, transfer)
    state, transfer, row_leaf = lax.optimization_barrier((state, transfer, row_leaf))
    for level in range(transfer.shape[1]):
        stacked = with_partner(state, "bfly", level % bit_count)
        matrix = transfer[0, level, 0] if level else first
        state = jnp.dot(matrix, stacked, preferred_element_type=jnp.float32)
        state = state.astype(jnp.bfloat16)
    start = count * 5 // 8 - 1
    order = [(i + start) % count for i in range(count)]
    owned = row_leaf.shape[2] // count
    tiles = partial_rows(state, row_leaf, start * owned).reshape(count, owned, -1)
    tiles = lax.all_to_all(tiles, "blk", 0, 0, axis_index_groups=[order], tiled=True)
    summed = jnp.sum(tiles.astype(jnp.float32), axis=0)
    return (summed * (1.0 / math.sqrt(count))).astype(jnp.bfloat16)[None]


def solution(mesh):
    placed = (
        P("blk", "bfly", None, None),
        P("blk", "bfly", None, None),
        P("blk", None, "bfly", None, None),
        P("blk", "bfly", None, None),
    )
    return jax.shard_map(
        local, mesh=mesh, in_specs=placed, out_specs=P("bfly", "blk", None), check_vma=False
    )
```

```python
import functools
import math

import jax
import jax.numpy as jnp
from jax import lax
from jax.experimental import pallas as pl
from jax.experimental.pallas import tpu as pltpu
from jax.sharding import PartitionSpec as P

VMEM = pl.BlockSpec(memory_space=pltpu.VMEM)
HBM = pl.BlockSpec(memory_space=pltpu.HBM)


def leaf_kernel(ports, leaf, transfer, state, first, ports_v, leaf_v, sems):
    copies = [
        pltpu.make_async_copy(leaf.at[0, 0], leaf_v, sems.at[0]),
        pltpu.make_async_copy(ports.at[0, 0], ports_v, sems.at[1]),
        pltpu.make_async_copy(transfer.at[0, 0, 0], first, sems.at[2]),
    ]
    for copy in copies:
        copy.start()
    copies[0].wait()
    copies[1].wait()
    state[...] = jnp.dot(
        leaf_v[...], ports_v[...], preferred_element_type=jnp.float32
    ).astype(state.dtype)
    copies[2].wait()


def leaf_state(ports, leaf, transfer):
    rank = leaf.shape[2]
    held = [
        pltpu.with_memory_space_constraint(x, pltpu.HBM) for x in (ports, leaf, transfer)
    ]
    return pl.pallas_call(
        leaf_kernel,
        out_shape=(
            jax.ShapeDtypeStruct((rank, ports.shape[3]), jnp.bfloat16),
            jax.ShapeDtypeStruct(transfer.shape[3:], jnp.bfloat16),
        ),
        in_specs=[HBM] * 3,
        out_specs=(VMEM, VMEM),
        scratch_shapes=[
            pltpu.VMEM(ports.shape[2:], jnp.bfloat16),
            pltpu.VMEM(leaf.shape[2:], jnp.bfloat16),
            pltpu.SemaphoreType.DMA((3,)),
        ],
        compiler_params=pltpu.CompilerParams(vmem_limit_bytes=8 << 20),
        name="leaf_state",
    )(*held)


def rows_kernel(order, state, leaf, out):
    owned = leaf.shape[2] // len(order)
    product = jnp.dot(leaf[0, 0], state[...], preferred_element_type=jnp.float32)
    for i, block in enumerate(order):
        rows = product[block * owned : (block + 1) * owned]
        out[i * owned : (i + 1) * owned] = rows.astype(out.dtype)


def partial_rows(state, leaf, order):
    return pl.pallas_call(
        functools.partial(rows_kernel, order),
        out_shape=jax.ShapeDtypeStruct((leaf.shape[2], state.shape[1]), jnp.bfloat16),
        in_specs=[VMEM, VMEM],
        out_specs=VMEM,
        compiler_params=pltpu.CompilerParams(vmem_limit_bytes=8 << 20),
        name="partial_rows",
    )(state, leaf)


def with_partner(array, axis, bit):
    pairs = [[i, i | 1 << bit] for i in range(lax.axis_size(axis)) if not i >> bit & 1]
    return lax.all_gather(array, axis, axis_index_groups=pairs, tiled=True)


def local(port_vectors, column_leaf, transfer, row_leaf):
    bit_count = lax.axis_size("bfly").bit_length() - 1
    count = lax.axis_size("blk")
    state, first = leaf_state(port_vectors, column_leaf, transfer)
    state, transfer, row_leaf = lax.optimization_barrier((state, transfer, row_leaf))
    for level in range(transfer.shape[1]):
        stacked = with_partner(state, "bfly", level % bit_count)
        matrix = transfer[0, level, 0] if level else first
        state = jnp.dot(matrix, stacked, preferred_element_type=jnp.float32)
        state = state.astype(jnp.bfloat16)
    start = count * 5 // 8 - 1
    order = [(start - x + 14 * i) % count for x in (0, 1) for i in range(count // 2)]
    owned = row_leaf.shape[2] // count
    tiles = partial_rows(state, row_leaf, order).reshape(count, owned, -1)
    tiles = lax.all_to_all(tiles, "blk", 0, 0, axis_index_groups=[order], tiled=True)
    summed = jnp.sum(tiles.astype(jnp.float32), axis=0)
    return (summed * (1.0 / math.sqrt(count))).astype(jnp.bfloat16)[None]


def solution(mesh):
    placed = (
        P("blk", "bfly", None, None),
        P("blk", "bfly", None, None),
        P("blk", None, "bfly", None, None),
        P("blk", "bfly", None, None),
    )
    return jax.shard_map(
        local, mesh=mesh, in_specs=placed, out_specs=P("bfly", "blk", None), check_vma=False
    )
```
